32 devices in a mesh: row: 4 (over x, core), col: 2 (over y), layer: 4 (over z).
Axes of the slice: x: 2, y: 2, z: 4, core: 2. Of those that a mesh axis runs over, the one named last changes fastest.
Arguments:
- a_tiles: bfloat16 [4, 128, 16, 128, 128], P('layer', 'row', 'col'), may hold values from 0.01 to 16, as said below
- a_mask: int32 [4, 128, 16], P('layer', 'row', 'col'), may hold values from 0 to 1, as said below
- b_tiles: bfloat16 [4, 16, 8, 128, 128], P('layer', 'row', 'col'), may hold values from 0.01 to 16, as said below
- b_mask: int32 [4, 16, 8], P('layer', 'row', 'col'), may hold values 0 or 1
Outputs:
- next_tiles: bfloat16 [128, 8, 128, 128], P(('row', 'layer'), 'col')
The draws below stay inside these ranges and needn't reach their ends.
Inputs may be any that keep to these rules, and one draw needn't show every extreme that they name: `a_tiles`: entries are positive. `b_tiles`: entries are positive. `a_mask`: each entry is 0 or 1; the share of ones differs between tile rows.
All inputs are finite; a program needn't handle non-finite values. No bound on the sum of `b_mask` on one device may be relied on, other than what follows from the above.
Results may differ from the reference program's by a relative error of at most 0.001.
Values may be sent and summed in bfloat16 or wider, within the bound.
No kernel may reach another device: no remote copies, remote signals or barrier semaphores. Data moves between devices by JAX's collectives and lax.ppermute only.
A program may use at most 128 MiB of HBM per device.

```python
import math
import jax
import jax.numpy as jnp
from jax import lax

TB = 128
INNER_L = 16
ROWS_T = 128
COLS_T = 8
N_LAYER = 4


def draw_a_tiles(key, part):
    first_key, second_key = jax.random.split(jax.random.fold_in(key, 11))
    tile_shape = (N_LAYER, ROWS_T, INNER_L, TB, TB)
    values = jnp.exp(jax.random.uniform(first_key, tile_shape, jnp.float32, math.log(0.01), 0.0))
    spread = 10.0
    scales = jnp.exp(jax.random.uniform(second_key, (1, ROWS_T, 1, TB, 1), jnp.float32, 0.0, math.log(spread)))
    return (values * scales).astype(jnp.bfloat16)


def draw_b_tiles(key, part):
    first_key, second_key = jax.random.split(jax.random.fold_in(key, 23))
    tile_shape = (N_LAYER, INNER_L, COLS_T, TB, TB)
    values = jnp.exp(jax.random.uniform(first_key, tile_shape, jnp.float32, math.log(0.01), 0.0))
    spread = 10.0
    scales = jnp.exp(jax.random.uniform(second_key, (1, 1, COLS_T, 1, TB), jnp.float32, 0.0, math.log(spread)))
    return (values * scales).astype(jnp.bfloat16)


def draw_a_mask(key, part):
    first_key, second_key = jax.random.split(jax.random.fold_in(key, 7))
    row_index = lax.broadcasted_iota(jnp.int32, (N_LAYER, ROWS_T, 1), 1)
    levels = 2 + 6 * row_index // ROWS_T + jax.random.randint(first_key, (N_LAYER, ROWS_T, 1), 0, 3)
    picked = jax.random.randint(second_key, (N_LAYER, ROWS_T, INNER_L), 0, 10)
    return (picked < levels).astype(jnp.int32)


def place_ends(entries, own_key, least, high):
    place = [jax.random.randint(jax.random.fold_in(own_key, axis), (), 0, length) for axis, length in enumerate(entries.shape)]
    longest = entries.shape.index(max(entries.shape))
    neighbour = place[:longest] + [(place[longest] + 1) % entries.shape[longest]] + place[longest + 1:]
    return entries.at[tuple(place)].set(least).at[tuple(neighbour)].set(high)


def setup_inputs(seed: int = 0) -> dict:
    seeds = jax.random.split(jax.random.key(seed), 5)
    return {
        "a_tiles": draw_a_tiles(jax.random.fold_in(seeds[4], 71), 0),
        "a_mask": draw_a_mask(jax.random.fold_in(seeds[4], 71), 0),
        "b_tiles": draw_b_tiles(jax.random.fold_in(seeds[4], 71), 0),
        "b_mask": place_ends((jax.random.randint(seeds[3], (N_LAYER, INNER_L, COLS_T), 0, 3) < 2).astype(jnp.int32), jax.random.fold_in(seeds[3], 1), 0, 1),
    }


def reference(a_tiles, a_mask, b_tiles, b_mask):
    a_eff = a_tiles * a_mask.astype(jnp.bfloat16)[..., None, None]
    b_eff = b_tiles * b_mask.astype(jnp.bfloat16)[..., None, None]

    def layer_step(running, layer_pair):
        left = layer_pair[0].astype(jnp.float32)
        right = layer_pair[1].astype(jnp.float32)
        return running + jnp.einsum("ikab,kjbc->ijac", left, right, precision=lax.Precision.HIGHEST), None

    initial = jnp.zeros((ROWS_T, COLS_T, TB, TB), jnp.float32)
    product, _ = lax.scan(layer_step, initial, (a_eff, b_eff))
    squared = product * product
    colsum = jnp.sum(squared, axis=(0, 2))
    scaled = (ROWS_T * TB) * squared / (colsum[None, :, None, :] + 1e-6)
    return scaled.astype(jnp.bfloat16)
```

```python
import functools
import jax
import jax.numpy as jnp
from jax import lax
from jax.experimental import pallas as pl
from jax.experimental.pallas import tpu as pltpu
from jax.sharding import PartitionSpec as P


CODE_ROWS = 16
STEPS = 65000.0
MIDDLE = 32767
LOG_STEP = 0.0027076061740622863


def general_body(a_tiles, a_mask, b_tiles, b_mask):
    a_eff = (a_tiles * a_mask.astype(jnp.bfloat16)[..., None, None])[0]
    b_eff = (b_tiles * b_mask.astype(jnp.bfloat16)[..., None, None])[0]
    row_tiles = a_eff.shape[0]
    tile_size = a_eff.shape[-1]
    b_whole = lax.all_gather(b_eff, "row", axis=0, tiled=True)
    product = jnp.einsum(
        "ikab,kjbc->ijac",
        lax.all_gather(a_eff, "col", axis=1, tiled=True),
        b_whole,
        preferred_element_type=jnp.float32,
    )
    rows_total = row_tiles * lax.axis_size("row") * tile_size
    owned = lax.psum_scatter(product, "layer", scatter_dimension=0, tiled=True)
    squared = owned * owned
    local_sums = jnp.sum(squared, axis=(0, 2))
    colsum = lax.psum(local_sums, ("row", "layer"))
    scaled = rows_total * squared / (colsum[None, :, None, :] + 1e-06)
    return scaled.astype(jnp.bfloat16)


def encode(p, tiles, tile, out_ref):
    p3 = p.reshape(tiles, tile, tile)
    top = jnp.maximum(jnp.max(p3, axis=1), 1e-30)
    code = jnp.ceil(jnp.log(top) * (1.0 / LOG_STEP))
    factor = jnp.exp(code * -LOG_STEP) * STEPS
    q = (p3 * factor[:, None, :] + 0.5).astype(jnp.int32) - MIDDLE
    out_ref[: tiles * tile, :] = q.reshape(tiles * tile, tile).astype(jnp.int16)
    pad = jnp.zeros((CODE_ROWS - tiles, tile), jnp.int32)
    out_ref[tiles * tile :, :] = jnp.concatenate([code.astype(jnp.int32), pad], axis=0).astype(jnp.int16)


def decode(ref, tiles, tile):
    code = ref[tiles * tile :, :].astype(jnp.int32)[:tiles].astype(jnp.float32)
    factor = jnp.exp(code * LOG_STEP) * (1.0 / STEPS)
    q = ref[: tiles * tile, :].astype(jnp.int32) + MIDDLE
    q3 = q.astype(jnp.float32).reshape(tiles, tile, tile)
    return (q3 * factor[:, None, :]).reshape(tiles * tile, tile)


def partial(shard, info_ref, mask_ref, a_ref, b_refs, partner):
    tiles, inner, tile = a_ref.shape[0], a_ref.shape[1], a_ref.shape[3]
    straight = (info_ref[1] != 0) != partner
    first = info_ref[2] == 0
    r_a, r_b, o_a, o_b = b_refs
    mine = jnp.where(straight, r_a[...], r_b[...])
    other = jnp.where(straight, o_a[...], o_b[...])
    low = jnp.where(first, mine, other)
    high = jnp.where(first, other, mine)
    right = jnp.concatenate([low, high], axis=0).reshape(inner * tile, tile)
    rows = []
    for i in range(tiles):
        base = (shard * tiles + i) * inner
        row = [
            jnp.where(mask_ref[base + k] != 0, a_ref[i, k], jnp.zeros((tile, tile), jnp.bfloat16))
            for k in range(inner)
        ]
        rows.append(jnp.concatenate(row, axis=1))
    left = jnp.concatenate(rows, axis=0)
    return jnp.dot(left, right, preferred_element_type=jnp.float32)


def send_kernel(info_ref, mask_ref, a_ref, ra, rb, oa, ob, out_ref):
    tiles, tile = a_ref.shape[0], a_ref.shape[3]
    p = partial(pl.program_id(0), info_ref, mask_ref, a_ref, (ra, rb, oa, ob), True)
    encode(p, tiles, tile, out_ref)


def keep_kernel(n_layer, info_ref, mask_ref, a_ref, ra, rb, oa, ob, in_ref, own_ref, *out_refs):
    tiles, tile = a_ref.shape[0], a_ref.shape[3]
    d = pl.program_id(0)
    shard = lax.rem(info_ref[0] + d, n_layer)
    p = partial(shard, info_ref, mask_ref, a_ref, (ra, rb, oa, ob), False)
    p = p + decode(in_ref, tiles, tile)

    @pl.when(d == 0)
    def _():
        own_ref[...] = p

    for e in range(1, n_layer):

        @pl.when(d == e)
        def _(e=e):
            encode(p, tiles, tile, out_refs[e - 1])


def sum_kernel(own_ref, *refs):
    ins, (sq_ref, cs_ref) = refs[:-2], refs[-2:]
    tile = own_ref.shape[1]
    tiles = own_ref.shape[0] // tile
    p = own_ref[...]
    for ref in ins:
        p = p + decode(ref, tiles, tile)
    sq = p * p
    sq_ref[...] = sq
    cs_ref[...] = jnp.sum(sq, axis=0, keepdims=True)


def final_kernel(rows_total, cs_ref, *refs):
    ins, out_ref = refs[:-1], refs[-1]
    tiles, _, tile, _ = out_ref.shape
    for j, ref in enumerate(ins):
        bottom = cs_ref[j : j + 1, :] + 1e-6
        out = (rows_total * ref[...]) / bottom
        out_ref[:, j] = out.reshape(tiles, tile, tile).astype(jnp.bfloat16)


def coded_body(n_row, n_layer, a_tiles, a_mask, b_tiles, b_mask):
    _, row_tiles, inner, tile, _ = a_tiles.shape
    cols = b_tiles.shape[2]
    tiles = row_tiles // n_layer
    rows_total = float(row_tiles * n_row * tile)
    row = lax.axis_index("row")
    col = lax.axis_index("col")
    layer = lax.axis_index("layer")
    half = row // 2
    core = row % 2
    info = jnp.stack([layer, (half == col).astype(jnp.int32), core]).astype(jnp.int32)
    mask = a_mask.reshape(-1)
    b_eff = (b_tiles * b_mask.astype(jnp.bfloat16)[..., None, None])[0]

    devices = [(x, k, y) for x in range(2) for k in range(2) for y in range(2)]
    number = lambda x, k, y: (x * 2 + k) * 2 + y
    turn_a = [(number(y, k, x), number(x, k, y)) for x, k, y in devices]
    turn_b = [(number(y, k, 1 - x), number(x, k, y)) for x, k, y in devices]
    swap_core = [(r, r ^ 1) for r in range(n_row)]
    swap_half = [(r, r ^ 2) for r in range(n_row)]
    swap_col = [(0, 1), (1, 0)]

    unit = tiles * tile + CODE_ROWS
    coded = jax.ShapeDtypeStruct((unit, tile), jnp.int16)
    b_spec = pl.BlockSpec((b_tiles.shape[1], tile, tile), lambda d, info, m: (0, 0, 0))
    flops = 2 * row_tiles * tile * inner * tile * tile
    cost = pl.CostEstimate(flops=flops, transcendentals=0, bytes_accessed=a_tiles.size * 2)

    send = pl.pallas_call(
        send_kernel,
        out_shape=jax.ShapeDtypeStruct((n_layer, unit, tile), jnp.int16),
        grid_spec=pltpu.PrefetchScalarGridSpec(
            num_scalar_prefetch=2,
            grid=(n_layer,),
            in_specs=[pl.BlockSpec((None, tiles, inner, tile, tile), lambda d, info, m: (0, d, 0, 0, 0))]
            + [b_spec] * 4,
            out_specs=pl.BlockSpec((None, unit, tile), lambda d, info, m: (d, 0, 0)),
        ),
        cost_estimate=cost,
        name="send",
    )
    shard_of = lambda d, info: lax.rem(info[0] + d, n_layer)
    keep = pl.pallas_call(
        functools.partial(keep_kernel, n_layer),
        out_shape=[jax.ShapeDtypeStruct((tiles * tile, tile), jnp.float32)] + [coded] * (n_layer - 1),
        grid_spec=pltpu.PrefetchScalarGridSpec(
            num_scalar_prefetch=2,
            grid=(n_layer,),
            in_specs=[
                pl.BlockSpec((None, tiles, inner, tile, tile), lambda d, info, m: (0, shard_of(d, info), 0, 0, 0))
            ]
            + [b_spec] * 4
            + [pl.BlockSpec((None, unit, tile), lambda d, info, m: (shard_of(d, info), 0, 0))],
            out_specs=[pl.BlockSpec((tiles * tile, tile), lambda d, info, m: (0, 0))]
            + [pl.BlockSpec((unit, tile), lambda d, info, m: (0, 0))] * (n_layer - 1),
        ),
        cost_estimate=cost,
        name="keep",
    )
    add = pl.pallas_call(
        sum_kernel,
        out_shape=[
            jax.ShapeDtypeStruct((tiles * tile, tile), jnp.float32),
            jax.ShapeDtypeStruct((1, tile), jnp.float32),
        ],
        name="add",
    )

    squares, sums = [], []
    for j in range(cols):
        b_j = b_eff[:, j]
        r_a = lax.ppermute(b_j, ("row", "col"), turn_a)
        r_b = lax.ppermute(b_j, ("row", "col"), turn_b)
        o_a = lax.ppermute(r_a, "row", swap_core)
        o_b = lax.ppermute(r_b, "row", swap_core)
        out = send(info, mask, a_tiles, r_a, r_b, o_a, o_b)
        arrived = lax.ppermute(out, "col", swap_col)
        own, *parts = keep(info, mask, a_tiles, r_a, r_b, o_a, o_b, arrived)
        got = [
            lax.ppermute(part, "layer", [(l, (l + d) % n_layer) for l in range(n_layer)])
            for d, part in enumerate(parts, 1)
        ]
        sq, cs = add(own, *got)
        squares.append(sq)
        sums.append(cs)
    colsum = jnp.concatenate(sums, axis=0)
    colsum = colsum + lax.ppermute(colsum, "row", swap_core)
    colsum = colsum + lax.ppermute(colsum, "row", swap_half)
    step = 1
    while step < n_layer:
        colsum = colsum + lax.ppermute(colsum, "layer", [(l, l ^ step) for l in range(n_layer)])
        step *= 2
    parts = 4
    return pl.pallas_call(
        functools.partial(final_kernel, rows_total),
        out_shape=jax.ShapeDtypeStruct((tiles, cols, tile, tile), jnp.bfloat16),
        grid=(parts,),
        in_specs=[pl.BlockSpec((cols, tile), lambda g: (0, 0))]
        + [pl.BlockSpec((tiles * tile // parts, tile), lambda g: (g, 0))] * cols,
        out_specs=pl.BlockSpec((tiles // parts, cols, tile, tile), lambda g: (g, 0, 0, 0)),
        name="final",
    )(colsum, *squares)


def solution(mesh):
    n_row, n_col, n_layer = mesh.shape["row"], mesh.shape["col"], mesh.shape["layer"]

    def body(a_tiles, a_mask, b_tiles, b_mask):
        row_tiles, inner = a_tiles.shape[1:3]
        tiles = row_tiles // n_layer
        fits = (
            n_row == 4
            and n_col == 2
            and n_layer & (n_layer - 1) == 0
            and inner == 2 * b_tiles.shape[1]
            and tiles * n_layer == row_tiles
            and tiles <= CODE_ROWS
            and tiles % 4 == 0
        )
        if fits:
            return coded_body(n_row, n_layer, a_tiles, a_mask, b_tiles, b_mask)
        return general_body(a_tiles, a_mask, b_tiles, b_mask)

    return jax.shard_map(
        body,
        mesh=mesh,
        in_specs=(
            P("layer", "row", "col", None, None),
            P("layer", "row", "col"),
            P("layer", "row", "col", None, None),
            P("layer", "row", "col"),
        ),
        out_specs=P(("row", "layer"), "col", None, None),
        check_vma=False,
    )
```

```python
import functools
import jax
import jax.numpy as jnp
from jax import lax
from jax.experimental import pallas as pl
from jax.experimental.pallas import tpu as pltpu
from jax.sharding import PartitionSpec as P


CODE_ROWS = 16
STEPS = 65000.0
MIDDLE = 32767
LOG_STEP = 0.0027076061740622863


VMEM = pl.BlockSpec(memory_space=pltpu.VMEM)
SMEM = pl.BlockSpec(memory_space=pltpu.SMEM)
LIMIT = pltpu.CompilerParams(vmem_limit_bytes=24 << 20)


def general_body(a_tiles, a_mask, b_tiles, b_mask):
    a_eff = (a_tiles * a_mask.astype(jnp.bfloat16)[..., None, None])[0]
    b_eff = (b_tiles * b_mask.astype(jnp.bfloat16)[..., None, None])[0]
    row_tiles = a_eff.shape[0]
    tile_size = a_eff.shape[-1]
    b_whole = lax.all_gather(b_eff, "row", axis=0, tiled=True)
    product = jnp.einsum(
        "ikab,kjbc->ijac",
        lax.all_gather(a_eff, "col", axis=1, tiled=True),
        b_whole,
        preferred_element_type=jnp.float32,
    )
    rows_total = row_tiles * lax.axis_size("row") * tile_size
    owned = lax.psum_scatter(product, "layer", scatter_dimension=0, tiled=True)
    squared = owned * owned
    local_sums = jnp.sum(squared, axis=(0, 2))
    colsum = lax.psum(local_sums, ("row", "layer"))
    scaled = rows_total * squared / (colsum[None, :, None, :] + 1e-06)
    return scaled.astype(jnp.bfloat16)


def encode(p, out_ref):
    rows, tile = p.shape
    tiles = rows // tile
    p3 = p.reshape(tiles, tile, tile)
    top = jnp.maximum(jnp.max(p3, axis=1), 1e-30)
    code = jnp.ceil(jnp.log(top) * (1.0 / LOG_STEP))
    factor = jnp.exp(code * -LOG_STEP) * STEPS
    q = (p3 * factor[:, None, :] + 0.5).astype(jnp.int32) - MIDDLE
    out_ref[:rows, :] = q.reshape(rows, tile).astype(jnp.int16)
    pad = jnp.zeros((CODE_ROWS - tiles, tile), jnp.int32)
    out_ref[rows:, :] = jnp.concatenate([code.astype(jnp.int32), pad], axis=0).astype(jnp.int16)


def decode(ref):
    tile = ref.shape[1]
    rows = ref.shape[0] - CODE_ROWS
    tiles = rows // tile
    code = ref[rows:, :].astype(jnp.int32)[:tiles].astype(jnp.float32)
    factor = jnp.exp(code * LOG_STEP) * (1.0 / STEPS)
    q = ref[:rows, :].astype(jnp.int32) + MIDDLE
    q3 = q.astype(jnp.float32).reshape(tiles, tile, tile)
    return (q3 * factor[:, None, :]).reshape(rows, tile)


def prepare_kernel(b_mask_ref, a_mask_ref, b_ref, a_ref, first_ref, rest_ref, low_ref, buffer, sems):
    shards, half = buffer.shape[:2]
    tiles = a_ref.shape[1] // shards
    copies = [
        pltpu.make_async_copy(a_ref.at[0, pl.ds(t * tiles, half)], buffer.at[t], sems.at[t]) for t in range(shards)
    ]
    for copy in copies:
        copy.start()
    _, inner, cols, tile, _ = b_ref.shape
    zero = jnp.zeros((tile, tile), jnp.bfloat16)
    for k in range(inner):
        for j in range(cols):
            value = jnp.where(b_mask_ref[k, j] != 0, b_ref[0, k, j], zero)
            if j == 0:
                first_ref[k] = value
            else:
                rest_ref[j - 1, k] = value
    for t, copy in enumerate(copies):
        copy.wait()
        mask_rows(a_mask_ref, t * tiles, buffer.at[t], low_ref.at[t])


def mask_rows(mask_ref, base, a_ref, out_ref):
    tiles, inner, tile = a_ref.shape[0], a_ref.shape[1], a_ref.shape[3]
    zero = jnp.zeros((tile, tile), jnp.bfloat16)
    for i in range(tiles):
        for k in range(inner):
            value = jnp.where(mask_ref[k, base + i] != 0, a_ref[i, k], zero)
            out_ref[i * tile : (i + 1) * tile, k * tile : (k + 1) * tile] = value


def mask_high_kernel(mask_ref, a_ref, out_ref):
    half = a_ref.shape[0]
    t = pl.program_id(0)
    mask_rows(mask_ref, (2 * t + 1) * half, a_ref, out_ref.at[t])


def right_side(b_refs, j):
    half, core = lax.axis_index("row") // 2, lax.axis_index("row") % 2
    straight = half == lax.axis_index("col")
    blocks = [ref[j] if j is not None else ref[...] for ref in b_refs]
    r_a, r_b, o_a, o_b = blocks
    sides = []
    for mine, other in (
        (jnp.where(straight, r_b, r_a), jnp.where(straight, o_b, o_a)),
        (jnp.where(straight, r_a, r_b), jnp.where(straight, o_a, o_b)),
    ):
        low = jnp.where(core == 0, mine, other)
        high = jnp.where(core == 0, other, mine)
        both = jnp.concatenate([low, high], axis=0)
        sides.append(both.reshape(both.shape[0] * both.shape[1], both.shape[2]))
    return jnp.concatenate(sides, axis=1)


def rows_of(parts, t):
    values = [ref[t, lo:hi, :] for ref, lo, hi in parts]
    return values[0] if len(values) == 1 else jnp.concatenate(values, axis=0)


def product_kernel(j, ranges, *refs):
    n = len(ranges)
    a_refs, b_refs, (out_ref, own_ref) = refs[:n], refs[n : n + 4], refs[n + 4 :]
    shards, _, tile = own_ref.shape
    right = right_side(b_refs, j)
    for t in range(shards):
        left = rows_of([(ref, lo, hi) for ref, (lo, hi) in zip(a_refs, ranges)], t)
        p = jnp.dot(left, right, preferred_element_type=jnp.float32)
        encode(p[:, :tile], out_ref.at[t])
        own_ref[t] = p[:, tile:]


def near_product_kernel(j, a_ref, *refs):
    b_refs, (keep_ref, out_ref) = refs[:4], refs[4:]
    tile = keep_ref.shape[2]
    layer = lax.axis_index("layer")
    right = right_side(b_refs, j)
    for step in range(a_ref.shape[0]):
        p = jnp.dot(a_ref[layer ^ step], right, preferred_element_type=jnp.float32)
        for side in range(2):
            value = p[:, side * tile : (side + 1) * tile]
            at = (step // 2) * 2 + side
            if step % 2:
                encode(value, out_ref.at[at])
            else:
                keep_ref[at] = value


def far_product_kernel(keep_ref, in_ref, own_ref, out_ref):
    for side in range(2):
        own_ref[side] = keep_ref[side] + decode(in_ref.at[side])
        encode(keep_ref[2 + side] + decode(in_ref.at[2 + side]), out_ref.at[side])


def finish_kernel(own_ref, in_ref, keep_ref, out_ref):
    encode(own_ref[0] + decode(in_ref.at[0]), out_ref)
    keep_ref[...] = own_ref[1] + decode(in_ref.at[1])


def split_kernel(own_ref, in_ref, keep_ref, out_ref):
    layer = lax.axis_index("layer")
    for n, step in enumerate((0, 2)):
        keep_ref[n] = own_ref[layer ^ step] + decode(in_ref.at[layer ^ step])
    for n, step in enumerate((1, 3)):
        encode(own_ref[layer ^ step] + decode(in_ref.at[layer ^ step]), out_ref.at[n])


def middle_kernel(keep_ref, in_ref, own_ref, out_ref):
    own_ref[...] = keep_ref[0] + decode(in_ref.at[0])
    encode(keep_ref[1] + decode(in_ref.at[1]), out_ref)


def direct_kernel(own_ref, in_ref, keep_ref, *out_refs):
    shards = own_ref.shape[0]
    layer = lax.axis_index("layer")
    for d, ref in enumerate(out_refs, 1):
        t = lax.rem(layer + d, shards)
        encode(own_ref[t] + decode(in_ref.at[t]), ref)
    keep_ref[...] = own_ref[layer] + decode(in_ref.at[layer])


def add_kernel(own_ref, *refs):
    ins, (sq_ref, cs_ref) = refs[:-2], refs[-2:]
    p = own_ref[...]
    for ref in ins:
        p = p + decode(ref)
    sq = p * p
    sq_ref[...] = sq
    cs_ref[...] = jnp.sum(sq, axis=0, keepdims=True)


def last_add_kernel(columns, own_ref, *refs):
    n_sums = len(columns) - 1
    ins, sums, (sq_ref, cs_ref) = refs[: -2 - n_sums], refs[-2 - n_sums : -2], refs[-2:]
    p = own_ref[...]
    for ref in ins:
        p = p + decode(ref)
    sq = p * p
    sq_ref[...] = sq
    totals = {}
    for column, value in zip(columns, [ref[...] for ref in sums] + [jnp.sum(sq, axis=0, keepdims=True)]):
        totals[column] = totals[column] + value if column in totals else value
    copies, height, tile = cs_ref.shape
    lines = [totals[column] for column in sorted(totals)]
    lines.append(jnp.zeros((height - len(lines), tile), jnp.float32))
    cs_ref[...] = jnp.broadcast_to(jnp.concatenate(lines, axis=0)[None], (copies, height, tile))


def final_kernel(units, rows_total, cs_ref, *refs):
    ins, (out_ref, buffer, sems) = refs[:-3], refs[-3:]
    tiles, _, tile, _ = out_ref.shape
    factor = rows_total / (jnp.sum(cs_ref[...], axis=0) + 1e-6)
    copies = []
    for i in range(tiles):
        for (j, lo, n), ref in zip(units, ins):
            if lo <= i < lo + n:
                value = ref[(i - lo) * tile : (i - lo + 1) * tile, :] * factor[j : j + 1, :]
                buffer[i, j] = value.astype(jnp.bfloat16)
        copies.append(pltpu.make_async_copy(buffer.at[i], out_ref.at[i], sems.at[i]))
        copies[-1].start()
    for copy in copies:
        copy.wait()


def coded_body(n_row, n_layer, a_tiles, a_mask, b_tiles, b_mask):
    _, row_tiles, inner, tile, _ = a_tiles.shape
    b_inner, cols = b_tiles.shape[1:3]
    tiles = row_tiles // n_layer
    rows_total = float(row_tiles * n_row * tile)
    f32, bf16, i16 = jnp.float32, jnp.bfloat16, jnp.int16
    shape = jax.ShapeDtypeStruct

    half, quarter, last_col = tiles // 2, tiles // 4, cols - 1
    units = {"0": (0, 0, half), "1": (1, 0, tiles), "2": (2, 0, half), "3": (2, half, half)}
    units |= {"4": (last_col, 0, half), "5": (last_col, half, quarter), "6": (last_col, half + quarter, quarter)}
    layer_first = (0, half, half)
    final = "6"

    devices = [(x, k, y) for x in range(2) for k in range(2) for y in range(2)]
    number = lambda x, k, y: (x * 2 + k) * 2 + y
    turn_a = [(number(y, k, x), number(x, k, y)) for x, k, y in devices]
    turn_b = [(number(y, k, 1 - x), number(x, k, y)) for x, k, y in devices]
    swap_core = [(r, r ^ 1) for r in range(n_row)]
    swap_col = [(0, 1), (1, 0)]
    pair = lambda step: [(l, l ^ step) for l in range(n_layer)]
    shift = lambda d: [(l, (l + d) % n_layer) for l in range(n_layer)]

    def call(kernel, outs, args, **extra):
        single = not isinstance(outs, list)
        return pl.pallas_call(
            kernel,
            out_shape=outs,
            in_specs=extra.pop("in_specs", [VMEM] * len(args)),
            out_specs=extra.pop("out_specs", VMEM if single else [VMEM] * len(outs)),
            compiler_params=LIMIT,
            **extra,
        )(*args)

    mask_t = a_mask[0].T
    b_first, b_rest, low = call(
        prepare_kernel,
        [
            shape((b_inner, tile, tile), bf16),
            shape((cols - 1, b_inner, tile, tile), bf16),
            shape((n_layer, half * tile, inner * tile), bf16),
        ],
        (b_mask[0], mask_t, b_tiles, a_tiles),
        in_specs=[SMEM, SMEM, VMEM, pl.BlockSpec(memory_space=pl.ANY)],
        scratch_shapes=[
            pltpu.VMEM((n_layer, half, inner, tile, tile), bf16),
            pltpu.SemaphoreType.DMA((n_layer,)),
        ],
    )

    def spread(block):
        r_a = lax.ppermute(block, ("row", "col"), turn_a)
        r_b = lax.ppermute(block, ("row", "col"), turn_b)
        return r_a, r_b

    def share(r_a, r_b):
        return r_a, r_b, lax.ppermute(r_a, "row", swap_core), lax.ppermute(r_b, "row", swap_core)

    turned = spread(b_first)
    turned_rest = spread(b_rest)
    first = share(*turned)
    rest = share(*turned_rest)

    def cost(rows):
        return pl.CostEstimate(
            flops=4 * n_layer * rows * inner * tile * tile,
            transcendentals=0,
            bytes_accessed=2 * n_layer * rows * inner * tile,
        )

    def batch(j):
        return (None, first) if j == 0 else (j - 1, rest)

    def product(unit):
        j, lo, n = unit
        at, blocks = batch(j)
        pieces = [(low, lo, min(lo + n, half)), (high, max(lo, half) - half, lo + n - half)]
        pieces = [(a, p * tile, q * tile) for a, p, q in pieces if a is not None and p < q]
        rows = n * tile
        return call(
            functools.partial(product_kernel, at, [piece[1:] for piece in pieces]),
            [shape((n_layer, rows + CODE_ROWS, tile), i16), shape((n_layer, rows, tile), f32)],
            [piece[0] for piece in pieces] + list(blocks),
            cost_estimate=cost(rows),
        )

    sent, own = {}, {}
    high = None
    coded, own["0"] = product(units["0"])
    sent["0"] = lax.ppermute(coded, "col", swap_col)
    late, _ = lax.optimization_barrier((a_tiles, coded))
    high = call(
        mask_high_kernel,
        shape((n_layer, half * tile, inner * tile), bf16),
        (mask_t, late),
        grid=(n_layer,),
        in_specs=[SMEM, pl.BlockSpec((None, half, inner, tile, tile), lambda t: (0, 2 * t + 1, 0, 0, 0))],
    )
    for u in list(units)[1:]:
        coded, own[u] = product(units[u])
        sent[u] = lax.ppermute(coded, "col", swap_col)

    squares, sums = {}, {}

    def add(u, kept, got):
        rows = kept.shape[0]
        last = u == final
        kernel, more, out = add_kernel, [], (1, tile)
        if last:
            order = list(sums)
            columns = [all_units[v][0] for v in order] + [all_units[u][0]]
            kernel, more = functools.partial(last_add_kernel, columns), [sums[v] for v in order]
            out = (n_row * n_layer, 8, tile)
        squares[u], sums[u] = call(kernel, [shape((rows, tile), f32), shape(out, f32)], [kept, *got, *more])

    all_units = units | {"z": layer_first}

    j, lo, n = layer_first
    rows = n * tile
    at, blocks = batch(j)
    kept, part = call(
        functools.partial(near_product_kernel, at),
        [shape((4, rows, tile), f32), shape((4, rows + CODE_ROWS, tile), i16)],
        [high, *blocks],
        cost_estimate=cost(rows),
    )
    part = lax.ppermute(part, "layer", pair(1))
    kept, part = call(
        far_product_kernel, [shape((2, rows, tile), f32), shape((2, rows + CODE_ROWS, tile), i16)], [kept, part]
    )
    part = lax.ppermute(part, "layer", pair(2))
    kept, part = call(finish_kernel, [shape((rows, tile), f32), shape((rows + CODE_ROWS, tile), i16)], [kept, part])
    add("z", kept, [lax.ppermute(part, "col", swap_col)])

    for u, (j, lo, n) in units.items():
        rows = n * tile
        block = shape((rows + CODE_ROWS, tile), i16)
        if u == final:
            kept, *parts = call(direct_kernel, [shape((rows, tile), f32)] + [block] * (n_layer - 1), [own[u], sent[u]])
            got = [lax.ppermute(part, "layer", shift(d)) for d, part in enumerate(parts, 1)]
        else:
            kept, part = call(
                split_kernel, [shape((2, rows, tile), f32), shape((2, rows + CODE_ROWS, tile), i16)], [own[u], sent[u]]
            )
            part = lax.ppermute(part, "layer", pair(1))
            kept, part = call(middle_kernel, [shape((rows, tile), f32), block], [kept, part])
            got = [lax.ppermute(part, "layer", pair(2))]
        add(u, kept, got)
    sums = sums[final]
    colsum = lax.all_to_all(sums, ("row", "layer"), 0, 0, tiled=True)
    return pl.pallas_call(
        functools.partial(final_kernel, [all_units[u] for u in squares], rows_total),
        out_shape=shape((tiles, cols, tile, tile), bf16),
        in_specs=[VMEM] * (1 + len(squares)),
        out_specs=pl.BlockSpec(memory_space=pl.ANY),
        scratch_shapes=[pltpu.VMEM((tiles, cols, tile, tile), bf16), pltpu.SemaphoreType.DMA((tiles,))],
        compiler_params=LIMIT,
        name="final",
    )(colsum, *squares.values())


def solution(mesh):
    n_row, n_col, n_layer = mesh.shape["row"], mesh.shape["col"], mesh.shape["layer"]

    def body(a_tiles, a_mask, b_tiles, b_mask):
        row_tiles, inner = a_tiles.shape[1:3]
        tiles = row_tiles // n_layer
        fits = (
            n_row == 4
            and n_col == 2
            and n_layer == 4
            and inner == 2 * b_tiles.shape[1]
            and tiles * n_layer == row_tiles
            and tiles <= CODE_ROWS
            and tiles % 4 == 0
            and b_tiles.shape[2] == 4
        )
        if fits:
            return coded_body(n_row, n_layer, a_tiles, a_mask, b_tiles, b_mask)
        return general_body(a_tiles, a_mask, b_tiles, b_mask)

    return jax.shard_map(
        body,
        mesh=mesh,
        in_specs=(
            P("layer", "row", "col", None, None),
            P("layer", "row", "col"),
            P("layer", "row", "col", None, None),
            P("layer", "row", "col"),
        ),
        out_specs=P(("row", "layer"), "col", None, None),
        check_vma=False,
    )
```

```python
import functools
import jax
import jax.numpy as jnp
from jax import lax
from jax.experimental import pallas as pl
from jax.experimental.pallas import tpu as pltpu
from jax.sharding import PartitionSpec as P


CODE_ROWS = 16
STEPS = 65000.0
MIDDLE = 32767
LOG_STEP = 0.0027076061740622863


VMEM = pl.BlockSpec(memory_space=pltpu.VMEM)
SMEM = pl.BlockSpec(memory_space=pltpu.SMEM)
LIMIT = pltpu.CompilerParams(vmem_limit_bytes=24 << 20)


def general_body(a_tiles, a_mask, b_tiles, b_mask):
    a_eff = (a_tiles * a_mask.astype(jnp.bfloat16)[..., None, None])[0]
    b_eff = (b_tiles * b_mask.astype(jnp.bfloat16)[..., None, None])[0]
    row_tiles = a_eff.shape[0]
    tile_size = a_eff.shape[-1]
    b_whole = lax.all_gather(b_eff, "row", axis=0, tiled=True)
    product = jnp.einsum(
        "ikab,kjbc->ijac",
        lax.all_gather(a_eff, "col", axis=1, tiled=True),
        b_whole,
        preferred_element_type=jnp.float32,
    )
    rows_total = row_tiles * lax.axis_size("row") * tile_size
    owned = lax.psum_scatter(product, "layer", scatter_dimension=0, tiled=True)
    squared = owned * owned
    local_sums = jnp.sum(squared, axis=(0, 2))
    colsum = lax.psum(local_sums, ("row", "layer"))
    scaled = rows_total * squared / (colsum[None, :, None, :] + 1e-06)
    return scaled.astype(jnp.bfloat16)


def encode(p, out_ref):
    rows, tile = p.shape
    tiles = rows // tile
    p3 = p.reshape(tiles, tile, tile)
    top = jnp.maximum(jnp.max(p3, axis=1), 1e-30)
    code = jnp.ceil(jnp.log(top) * (1.0 / LOG_STEP))
    factor = jnp.exp(code * -LOG_STEP) * STEPS
    q = (p3 * factor[:, None, :] + 0.5).astype(jnp.int32) - MIDDLE
    out_ref[:rows, :] = q.reshape(rows, tile).astype(jnp.int16)
    pad = jnp.zeros((CODE_ROWS - tiles, tile), jnp.int32)
    out_ref[rows:, :] = jnp.concatenate([code.astype(jnp.int32), pad], axis=0).astype(jnp.int16)


def decode(ref):
    tile = ref.shape[1]
    rows = ref.shape[0] - CODE_ROWS
    tiles = rows // tile
    code = ref[rows:, :].astype(jnp.int32)[:tiles].astype(jnp.float32)
    factor = jnp.exp(code * LOG_STEP) * (1.0 / STEPS)
    q = ref[:rows, :].astype(jnp.int32) + MIDDLE
    q3 = q.astype(jnp.float32).reshape(tiles, tile, tile)
    return (q3 * factor[:, None, :]).reshape(rows, tile)


def prepare_kernel(
    b_mask_ref, a_mask_ref, b_ref, a_ref, first_ref, rest_ref, low_ref, b_ones, a_ones, b_buffer, buffer, sems
):
    shards, half = buffer.shape[:2]
    tiles = a_ref.shape[1] // shards
    pairs = [(b_mask_ref, b_ones), (b_ref, b_buffer), (a_mask_ref, a_ones)]
    pairs += [(a_ref.at[0, pl.ds(t * tiles, half)], buffer.at[t]) for t in range(shards)]
    copies = [pltpu.make_async_copy(source, target, sems.at[n]) for n, (source, target) in enumerate(pairs)]
    for copy in copies:
        copy.start()
    _, inner, cols, tile, _ = b_ref.shape
    zero = jnp.zeros((tile, tile), jnp.bfloat16)
    copies[0].wait()
    copies[1].wait()
    for k in range(inner):
        for j in range(cols):
            value = jnp.where(b_ones[k, j] != 0, b_buffer[0, k, j], zero)
            if j == 0:
                first_ref[k] = value
            else:
                rest_ref[j - 1, k] = value
    copies[2].wait()
    for t, copy in enumerate(copies[3:]):
        copy.wait()
        mask_rows(a_ones, t * tiles, buffer.at[t], low_ref.at[t])


def mask_rows(mask_ref, base, a_ref, out_ref):
    tiles, inner, tile = a_ref.shape[0], a_ref.shape[1], a_ref.shape[3]
    zero = jnp.zeros((tile, tile), jnp.bfloat16)
    for i in range(tiles):
        for k in range(inner):
            value = jnp.where(mask_ref[k, base + i] != 0, a_ref[i, k], zero)
            out_ref[i * tile : (i + 1) * tile, k * tile : (k + 1) * tile] = value


def mask_high_kernel(mask_ref, a_ref, out_ref):
    half = a_ref.shape[0]
    t = pl.program_id(0)
    mask_rows(mask_ref, (2 * t + 1) * half, a_ref, out_ref.at[t])


def right_side(b_refs, j):
    half, core = lax.axis_index("row") // 2, lax.axis_index("row") % 2
    straight = half == lax.axis_index("col")
    blocks = [ref[j] if j is not None else ref[...] for ref in b_refs]
    r_a, r_b, o_a, o_b = blocks
    sides = []
    for mine, other in (
        (jnp.where(straight, r_b, r_a), jnp.where(straight, o_b, o_a)),
        (jnp.where(straight, r_a, r_b), jnp.where(straight, o_a, o_b)),
    ):
        low = jnp.where(core == 0, mine, other)
        high = jnp.where(core == 0, other, mine)
        both = jnp.concatenate([low, high], axis=0)
        sides.append(both.reshape(both.shape[0] * both.shape[1], both.shape[2]))
    return jnp.concatenate(sides, axis=1)


def rows_of(parts, t):
    values = [ref[t, lo:hi, :] for ref, lo, hi in parts]
    return values[0] if len(values) == 1 else jnp.concatenate(values, axis=0)


def product_kernel(j, ranges, *refs):
    n = len(ranges)
    a_refs, b_refs, (out_ref, own_ref) = refs[:n], refs[n : n + 4], refs[n + 4 :]
    shards, _, tile = own_ref.shape
    right = right_side(b_refs, j)
    for t in range(shards):
        left = rows_of([(ref, lo, hi) for ref, (lo, hi) in zip(a_refs, ranges)], t)
        p = jnp.dot(left, right, preferred_element_type=jnp.float32)
        encode(p[:, :tile], out_ref.at[t])
        own_ref[t] = p[:, tile:]


def near_product_kernel(j, a_ref, *refs):
    b_refs, (keep_ref, out_ref) = refs[:4], refs[4:]
    tile = keep_ref.shape[2]
    layer = lax.axis_index("layer")
    right = right_side(b_refs, j)
    for step in range(a_ref.shape[0]):
        p = jnp.dot(a_ref[layer ^ step], right, preferred_element_type=jnp.float32)
        for side in range(2):
            value = p[:, side * tile : (side + 1) * tile]
            at = (step // 2) * 2 + side
            if step % 2:
                encode(value, out_ref.at[at])
            else:
                keep_ref[at] = value


def far_product_kernel(keep_ref, in_ref, own_ref, out_ref):
    for side in range(2):
        own_ref[side] = keep_ref[side] + decode(in_ref.at[side])
        encode(keep_ref[2 + side] + decode(in_ref.at[2 + side]), out_ref.at[side])


def finish_kernel(own_ref, in_ref, keep_ref, out_ref):
    encode(own_ref[0] + decode(in_ref.at[0]), out_ref)
    keep_ref[...] = own_ref[1] + decode(in_ref.at[1])


def split_kernel(own_ref, in_ref, keep_ref, out_ref):
    layer = lax.axis_index("layer")
    for n, step in enumerate((0, 2)):
        keep_ref[n] = own_ref[layer ^ step] + decode(in_ref.at[layer ^ step])
    for n, step in enumerate((1, 3)):
        encode(own_ref[layer ^ step] + decode(in_ref.at[layer ^ step]), out_ref.at[n])


def middle_kernel(keep_ref, in_ref, own_ref, out_ref):
    own_ref[...] = keep_ref[0] + decode(in_ref.at[0])
    encode(keep_ref[1] + decode(in_ref.at[1]), out_ref)


def direct_kernel(own_ref, in_ref, keep_ref, *out_refs):
    shards = own_ref.shape[0]
    layer = lax.axis_index("layer")
    for d, ref in enumerate(out_refs, 1):
        t = lax.rem(layer + d, shards)
        encode(own_ref[t] + decode(in_ref.at[t]), ref)
    keep_ref[...] = own_ref[layer] + decode(in_ref.at[layer])


def add_kernel(own_ref, *refs):
    ins, (sq_ref, cs_ref) = refs[:-2], refs[-2:]
    p = own_ref[...]
    for ref in ins:
        p = p + decode(ref)
    sq = p * p
    sq_ref[...] = sq
    cs_ref[...] = jnp.sum(sq, axis=0, keepdims=True)


def last_add_kernel(columns, own_ref, *refs):
    n_sums = len(columns) - 1
    ins, sums, (sq_ref, cs_ref) = refs[: -2 - n_sums], refs[-2 - n_sums : -2], refs[-2:]
    p = own_ref[...]
    for ref in ins:
        p = p + decode(ref)
    sq = p * p
    sq_ref[...] = sq
    totals = {}
    for column, value in zip(columns, [ref[...] for ref in sums] + [jnp.sum(sq, axis=0, keepdims=True)]):
        totals[column] = totals[column] + value if column in totals else value
    copies, height, tile = cs_ref.shape
    lines = [totals[column] for column in sorted(totals)]
    lines.append(jnp.zeros((height - len(lines), tile), jnp.float32))
    cs_ref[...] = jnp.broadcast_to(jnp.concatenate(lines, axis=0)[None], (copies, height, tile))


def final_kernel(units, rows_total, cs_ref, *refs):
    ins, (out_ref, buffer, sems) = refs[:-3], refs[-3:]
    tiles, _, tile, _ = out_ref.shape
    factor = rows_total / (jnp.sum(cs_ref[...], axis=0) + 1e-6)
    copies = []
    for i in range(tiles):
        for (j, lo, n), ref in zip(units, ins):
            if lo <= i < lo + n:
                value = ref[(i - lo) * tile : (i - lo + 1) * tile, :] * factor[j : j + 1, :]
                buffer[i, j] = value.astype(jnp.bfloat16)
        copies.append(pltpu.make_async_copy(buffer.at[i], out_ref.at[i], sems.at[i]))
        copies[-1].start()
    for copy in copies:
        copy.wait()


def coded_body(n_row, n_layer, a_tiles, a_mask, b_tiles, b_mask):
    _, row_tiles, inner, tile, _ = a_tiles.shape
    b_inner, cols = b_tiles.shape[1:3]
    tiles = row_tiles // n_layer
    rows_total = float(row_tiles * n_row * tile)
    f32, bf16, i16 = jnp.float32, jnp.bfloat16, jnp.int16
    shape = jax.ShapeDtypeStruct

    half, quarter, last_col = tiles // 2, tiles // 4, cols - 1
    units = {"0": (0, 0, half)}
    for j in range(1, last_col):
        units |= {str(2 * j - 1): (j, 0, half), str(2 * j): (j, half, half)}
    units |= {"5": (last_col, 0, half), "6": (last_col, half, quarter), "7": (last_col, half + quarter, quarter)}
    layer_first = (0, half, half)
    final = "7"

    devices = [(x, k, y) for x in range(2) for k in range(2) for y in range(2)]
    number = lambda x, k, y: (x * 2 + k) * 2 + y
    turn_a = [(number(y, k, x), number(x, k, y)) for x, k, y in devices]
    turn_b = [(number(y, k, 1 - x), number(x, k, y)) for x, k, y in devices]
    swap_core = [(r, r ^ 1) for r in range(n_row)]
    swap_col = [(0, 1), (1, 0)]
    pair = lambda step: [(l, l ^ step) for l in range(n_layer)]
    shift = lambda d: [(l, (l + d) % n_layer) for l in range(n_layer)]

    def call(kernel, outs, args, **extra):
        single = not isinstance(outs, list)
        return pl.pallas_call(
            kernel,
            out_shape=outs,
            in_specs=extra.pop("in_specs", [VMEM] * len(args)),
            out_specs=extra.pop("out_specs", VMEM if single else [VMEM] * len(outs)),
            compiler_params=LIMIT,
            **extra,
        )(*args)

    mask_t = a_mask[0].T
    b_first, b_rest, low = call(
        prepare_kernel,
        [
            shape((b_inner, tile, tile), bf16),
            shape((cols - 1, b_inner, tile, tile), bf16),
            shape((n_layer, half * tile, inner * tile), bf16),
        ],
        [pltpu.with_memory_space_constraint(x, pltpu.HBM) for x in (b_mask[0], mask_t, b_tiles, a_tiles)],
        in_specs=[pl.BlockSpec(memory_space=pltpu.HBM)] * 4,
        scratch_shapes=[
            pltpu.SMEM(b_mask.shape[1:], jnp.int32),
            pltpu.SMEM(mask_t.shape, jnp.int32),
            pltpu.VMEM(b_tiles.shape, bf16),
            pltpu.VMEM((n_layer, half, inner, tile, tile), bf16),
            pltpu.SemaphoreType.DMA((3 + n_layer,)),
        ],
    )

    def spread(block):
        r_a = lax.ppermute(block, ("row", "col"), turn_a)
        r_b = lax.ppermute(block, ("row", "col"), turn_b)
        return r_a, r_b

    def share(r_a, r_b):
        return r_a, r_b, lax.ppermute(r_a, "row", swap_core), lax.ppermute(r_b, "row", swap_core)

    turned = spread(b_first)
    turned_rest = spread(b_rest)
    first = share(*turned)
    rest = share(*turned_rest)

    def cost(rows):
        return pl.CostEstimate(
            flops=4 * n_layer * rows * inner * tile * tile,
            transcendentals=0,
            bytes_accessed=2 * n_layer * rows * inner * tile,
        )

    def batch(j):
        return (None, first) if j == 0 else (j - 1, rest)

    def product(unit):
        j, lo, n = unit
        at, blocks = batch(j)
        pieces = [(low, lo, min(lo + n, half)), (high, max(lo, half) - half, lo + n - half)]
        pieces = [(a, p * tile, q * tile) for a, p, q in pieces if a is not None and p < q]
        rows = n * tile
        return call(
            functools.partial(product_kernel, at, [piece[1:] for piece in pieces]),
            [shape((n_layer, rows + CODE_ROWS, tile), i16), shape((n_layer, rows, tile), f32)],
            [piece[0] for piece in pieces] + list(blocks),
            cost_estimate=cost(rows),
        )

    sent, own = {}, {}
    high = None
    coded, own["0"] = product(units["0"])
    sent["0"] = lax.ppermute(coded, "col", swap_col)
    late, _ = lax.optimization_barrier((a_tiles, coded))
    high = call(
        mask_high_kernel,
        shape((n_layer, half * tile, inner * tile), bf16),
        (mask_t, late),
        grid=(n_layer,),
        in_specs=[SMEM, pl.BlockSpec((None, half, inner, tile, tile), lambda t: (0, 2 * t + 1, 0, 0, 0))],
    )
    for u in list(units)[1:]:
        coded, own[u] = product(units[u])
        sent[u] = lax.ppermute(coded, "col", swap_col)

    squares, sums = {}, {}

    def add(u, kept, got):
        rows = kept.shape[0]
        last = u == final
        kernel, more, out = add_kernel, [], (1, tile)
        if last:
            order = list(sums)
            columns = [all_units[v][0] for v in order] + [all_units[u][0]]
            kernel, more = functools.partial(last_add_kernel, columns), [sums[v] for v in order]
            out = (n_row * n_layer, 8, tile)
        squares[u], sums[u] = call(kernel, [shape((rows, tile), f32), shape(out, f32)], [kept, *got, *more])

    all_units = units | {"z": layer_first}

    j, lo, n = layer_first
    rows = n * tile
    at, blocks = batch(j)
    kept, part = call(
        functools.partial(near_product_kernel, at),
        [shape((4, rows, tile), f32), shape((4, rows + CODE_ROWS, tile), i16)],
        [high, *blocks],
        cost_estimate=cost(rows),
    )
    part = lax.ppermute(part, "layer", pair(1))
    kept, part = call(
        far_product_kernel, [shape((2, rows, tile), f32), shape((2, rows + CODE_ROWS, tile), i16)], [kept, part]
    )
    part = lax.ppermute(part, "layer", pair(2))
    kept, part = call(finish_kernel, [shape((rows, tile), f32), shape((rows + CODE_ROWS, tile), i16)], [kept, part])
    add("z", kept, [lax.ppermute(part, "col", swap_col)])

    for u, (j, lo, n) in units.items():
        rows = n * tile
        block = shape((rows + CODE_ROWS, tile), i16)
        if u == final:
            kept, *parts = call(direct_kernel, [shape((rows, tile), f32)] + [block] * (n_layer - 1), [own[u], sent[u]])
            got = [lax.ppermute(part, "layer", shift(d)) for d, part in enumerate(parts, 1)]
        else:
            kept, part = call(
                split_kernel, [shape((2, rows, tile), f32), shape((2, rows + CODE_ROWS, tile), i16)], [own[u], sent[u]]
            )
            part = lax.ppermute(part, "layer", pair(1))
            kept, part = call(middle_kernel, [shape((rows, tile), f32), block], [kept, part])
            got = [lax.ppermute(part, "layer", pair(2))]
        add(u, kept, got)
    sums = sums[final]
    colsum = lax.all_to_all(sums, ("row", "layer"), 0, 0, tiled=True)
    return pl.pallas_call(
        functools.partial(final_kernel, [all_units[u] for u in squares], rows_total),
        out_shape=shape((tiles, cols, tile, tile), bf16),
        in_specs=[VMEM] * (1 + len(squares)),
        out_specs=pl.BlockSpec(memory_space=pl.ANY),
        scratch_shapes=[pltpu.VMEM((tiles, cols, tile, tile), bf16), pltpu.SemaphoreType.DMA((tiles,))],
        compiler_params=LIMIT,
        name="final",
    )(colsum, *squares.values())


def solution(mesh):
    n_row, n_col, n_layer = mesh.shape["row"], mesh.shape["col"], mesh.shape["layer"]

    def body(a_tiles, a_mask, b_tiles, b_mask):
        row_tiles, inner = a_tiles.shape[1:3]
        tiles = row_tiles // n_layer
        fits = (
            n_row == 4
            and n_col == 2
            and n_layer == 4
            and inner == 2 * b_tiles.shape[1]
            and tiles * n_layer == row_tiles
            and tiles <= CODE_ROWS
            and tiles % 4 == 0
            and b_tiles.shape[2] == 4
        )
        if fits:
            return coded_body(n_row, n_layer, a_tiles, a_mask, b_tiles, b_mask)
        return general_body(a_tiles, a_mask, b_tiles, b_mask)

    return jax.shard_map(
        body,
        mesh=mesh,
        in_specs=(
            P("layer", "row", "col", None, None),
            P("layer", "row", "col"),
            P("layer", "row", "col", None, None),
            P("layer", "row", "col"),
        ),
        out_specs=P(("row", "layer"), "col", None, None),
        check_vma=False,
    )
```

```python
import functools
import jax
import jax.numpy as jnp
from jax import lax
from jax.experimental import pallas as pl
from jax.experimental.pallas import tpu as pltpu
from jax.sharding import PartitionSpec as P


CODE_ROWS = 8
STEPS = 65000.0
MIDDLE = 32767
LOG_STEP = 0.0027076061740622863


VMEM = pl.BlockSpec(memory_space=pltpu.VMEM)
SMEM = pl.BlockSpec(memory_space=pltpu.SMEM)
LIMIT = pltpu.CompilerParams(vmem_limit_bytes=24 << 20)


def general_body(a_tiles, a_mask, b_tiles, b_mask):
    a_eff = (a_tiles * a_mask.astype(jnp.bfloat16)[..., None, None])[0]
    b_eff = (b_tiles * b_mask.astype(jnp.bfloat16)[..., None, None])[0]
    row_tiles = a_eff.shape[0]
    tile_size = a_eff.shape[-1]
    b_whole = lax.all_gather(b_eff, "row", axis=0, tiled=True)
    product = jnp.einsum(
        "ikab,kjbc->ijac",
        lax.all_gather(a_eff, "col", axis=1, tiled=True),
        b_whole,
        preferred_element_type=jnp.float32,
    )
    rows_total = row_tiles * lax.axis_size("row") * tile_size
    owned = lax.psum_scatter(product, "layer", scatter_dimension=0, tiled=True)
    squared = owned * owned
    local_sums = jnp.sum(squared, axis=(0, 2))
    colsum = lax.psum(local_sums, ("row", "layer"))
    scaled = rows_total * squared / (colsum[None, :, None, :] + 1e-06)
    return scaled.astype(jnp.bfloat16)


def encode(p, out_ref):
    rows, tile = p.shape
    tiles = rows // tile
    p3 = p.reshape(tiles, tile, tile)
    top = jnp.maximum(jnp.max(p3, axis=1), 1e-30)
    code = jnp.ceil(jnp.log(top) * (1.0 / LOG_STEP))
    factor = jnp.exp(code * -LOG_STEP) * STEPS
    q = (p3 * factor[:, None, :] + 0.5).astype(jnp.int32) - MIDDLE
    out_ref[:rows, :] = q.reshape(rows, tile).astype(jnp.int16)
    code = code.astype(jnp.int32)
    if tiles < CODE_ROWS:
        code = jnp.concatenate([code, jnp.zeros((CODE_ROWS - tiles, tile), jnp.int32)], axis=0)
    out_ref[rows:, :] = code.astype(jnp.int16)


def decode(ref):
    tile = ref.shape[1]
    rows = ref.shape[0] - CODE_ROWS
    tiles = rows // tile
    code = ref[rows:, :].astype(jnp.int32)[:tiles].astype(jnp.float32)
    factor = jnp.exp(code * LOG_STEP) * (1.0 / STEPS)
    q = ref[:rows, :].astype(jnp.int32) + MIDDLE
    q3 = q.astype(jnp.float32).reshape(tiles, tile, tile)
    return (q3 * factor[:, None, :]).reshape(rows, tile)


def prepare_kernel(
    b_mask_ref, a_mask_ref, b_ref, a_ref, first_ref, rest_ref, low_ref, b_ones, a_ones, b_buffer, buffer, sems
):
    shards, half = buffer.shape[:2]
    tiles = a_ref.shape[1] // shards
    pairs = [(b_mask_ref, b_ones), (b_ref, b_buffer), (a_mask_ref, a_ones)]
    pairs += [(a_ref.at[0, pl.ds(t * tiles, half)], buffer.at[t]) for t in range(shards)]
    copies = [pltpu.make_async_copy(source, target, sems.at[n]) for n, (source, target) in enumerate(pairs)]
    for copy in copies:
        copy.start()
    _, inner, cols, tile, _ = b_ref.shape
    zero = jnp.zeros((tile, tile), jnp.bfloat16)
    copies[0].wait()
    copies[1].wait()
    for k in range(inner):
        for j in range(cols):
            value = jnp.where(b_ones[k, j] != 0, b_buffer[0, k, j], zero)
            if j == 0:
                first_ref[k] = value
            else:
                rest_ref[j - 1, k] = value
    copies[2].wait()
    for t, copy in enumerate(copies[3:]):
        copy.wait()
        mask_rows(a_ones, t * tiles, buffer.at[t], low_ref.at[t])


def mask_rows(mask_ref, base, a_ref, out_ref):
    tiles, inner, tile = a_ref.shape[0], a_ref.shape[1], a_ref.shape[3]
    zero = jnp.zeros((tile, tile), jnp.bfloat16)
    for i in range(tiles):
        for k in range(inner):
            value = jnp.where(mask_ref[k, base + i] != 0, a_ref[i, k], zero)
            out_ref[i * tile : (i + 1) * tile, k * tile : (k + 1) * tile] = value


def mask_high_kernel(mask_ref, a_ref, out_ref):
    half = a_ref.shape[0]
    t = pl.program_id(0)
    mask_rows(mask_ref, (2 * t + 1) * half, a_ref, out_ref.at[t])


def right_side(b_refs, j):
    half, core = lax.axis_index("row") // 2, lax.axis_index("row") % 2
    straight = half == lax.axis_index("col")
    blocks = [ref[j] if j is not None else ref[...] for ref in b_refs]
    r_a, r_b, o_a, o_b = blocks
    sides = []
    for mine, other in (
        (jnp.where(straight, r_b, r_a), jnp.where(straight, o_b, o_a)),
        (jnp.where(straight, r_a, r_b), jnp.where(straight, o_a, o_b)),
    ):
        low = jnp.where(core == 0, mine, other)
        high = jnp.where(core == 0, other, mine)
        both = jnp.concatenate([low, high], axis=0)
        sides.append(both.reshape(both.shape[0] * both.shape[1], both.shape[2]))
    return jnp.concatenate(sides, axis=1)


def rows_of(parts, t):
    values = [ref[t, lo:hi, :] for ref, lo, hi in parts]
    return values[0] if len(values) == 1 else jnp.concatenate(values, axis=0)


def product_kernel(j, ranges, *refs):
    n = len(ranges)
    a_refs, b_refs, (out_ref, own_ref) = refs[:n], refs[n : n + 4], refs[n + 4 :]
    shards, _, tile = own_ref.shape
    right = right_side(b_refs, j)
    for t in range(shards):
        left = rows_of([(ref, lo, hi) for ref, (lo, hi) in zip(a_refs, ranges)], t)
        p = jnp.dot(left, right, preferred_element_type=jnp.float32)
        encode(p[:, :tile], out_ref.at[t])
        own_ref[t] = p[:, tile:]


def near_product_kernel(j, a_ref, *refs):
    b_refs, (keep_ref, out_ref) = refs[:4], refs[4:]
    tile = keep_ref.shape[2]
    layer = lax.axis_index("layer")
    right = right_side(b_refs, j)
    for step in range(a_ref.shape[0]):
        p = jnp.dot(a_ref[layer ^ step], right, preferred_element_type=jnp.float32)
        for side in range(2):
            value = p[:, side * tile : (side + 1) * tile]
            at = (step // 2) * 2 + side
            if step % 2:
                encode(value, out_ref.at[at])
            else:
                keep_ref[at] = value


def far_product_kernel(keep_ref, in_ref, own_ref, out_ref):
    for side in range(2):
        own_ref[side] = keep_ref[side] + decode(in_ref.at[side])
        encode(keep_ref[2 + side] + decode(in_ref.at[2 + side]), out_ref.at[side])


def finish_kernel(own_ref, in_ref, keep_ref, out_ref):
    encode(own_ref[0] + decode(in_ref.at[0]), out_ref)
    keep_ref[...] = own_ref[1] + decode(in_ref.at[1])


def split_kernel(own_ref, in_ref, keep_ref, out_ref):
    layer = lax.axis_index("layer")
    for n, step in enumerate((0, 2)):
        keep_ref[n] = own_ref[layer ^ step] + decode(in_ref.at[layer ^ step])
    for n, step in enumerate((1, 3)):
        encode(own_ref[layer ^ step] + decode(in_ref.at[layer ^ step]), out_ref.at[n])


def middle_kernel(keep_ref, in_ref, own_ref, out_ref):
    own_ref[...] = keep_ref[0] + decode(in_ref.at[0])
    encode(keep_ref[1] + decode(in_ref.at[1]), out_ref)


def direct_kernel(own_ref, in_ref, keep_ref, *out_refs):
    shards = own_ref.shape[0]
    layer = lax.axis_index("layer")
    for d, ref in enumerate(out_refs, 1):
        t = lax.rem(layer + d, shards)
        encode(own_ref[t] + decode(in_ref.at[t]), ref)
    keep_ref[...] = own_ref[layer] + decode(in_ref.at[layer])


def add_kernel(own_ref, *refs):
    ins, (sq_ref, cs_ref) = refs[:-2], refs[-2:]
    p = own_ref[...]
    for ref in ins:
        p = p + decode(ref)
    sq = p * p
    sq_ref[...] = sq
    cs_ref[...] = jnp.sum(sq, axis=0, keepdims=True)


def last_add_kernel(columns, own_ref, *refs):
    n_sums = len(columns) - 1
    ins, sums, (sq_ref, cs_ref) = refs[: -2 - n_sums], refs[-2 - n_sums : -2], refs[-2:]
    p = own_ref[...]
    for ref in ins:
        p = p + decode(ref)
    sq = p * p
    sq_ref[...] = sq
    totals = {}
    for column, value in zip(columns, [ref[...] for ref in sums] + [jnp.sum(sq, axis=0, keepdims=True)]):
        totals[column] = totals[column] + value if column in totals else value
    copies, height, tile = cs_ref.shape
    lines = [totals[column] for column in sorted(totals)]
    lines.append(jnp.zeros((height - len(lines), tile), jnp.float32))
    cs_ref[...] = jnp.broadcast_to(jnp.concatenate(lines, axis=0)[None], (copies, height, tile))


def final_kernel(units, rows_total, cs_ref, *refs):
    ins, (out_ref, buffer, sems) = refs[:-3], refs[-3:]
    tiles, _, tile, _ = out_ref.shape
    factor = rows_total / (jnp.sum(cs_ref[...], axis=0) + 1e-6)
    copies = []
    for i in range(tiles):
        for (j, lo, n), ref in zip(units, ins):
            if lo <= i < lo + n:
                value = ref[(i - lo) * tile : (i - lo + 1) * tile, :] * factor[j : j + 1, :]
                buffer[i, j] = value.astype(jnp.bfloat16)
        copies.append(pltpu.make_async_copy(buffer.at[i], out_ref.at[i], sems.at[i]))
        copies[-1].start()
    for copy in copies:
        copy.wait()


def coded_body(n_row, n_layer, a_tiles, a_mask, b_tiles, b_mask):
    _, row_tiles, inner, tile, _ = a_tiles.shape
    b_inner, cols = b_tiles.shape[1:3]
    tiles = row_tiles // n_layer
    rows_total = float(row_tiles * n_row * tile)
    f32, bf16, i16 = jnp.float32, jnp.bfloat16, jnp.int16
    shape = jax.ShapeDtypeStruct

    half, quarter, last_col = tiles // 2, tiles // 4, cols - 1
    units = {"0": (0, 0, half)}
    for j in range(1, last_col):
        units |= {str(2 * j - 1): (j, 0, half), str(2 * j): (j, half, half)}
    units |= {str(5 + q): (last_col, q * quarter, quarter) for q in range(4)}
    layer_first = (0, half, half)
    final = "8"

    devices = [(x, k, y) for x in range(2) for k in range(2) for y in range(2)]
    number = lambda x, k, y: (x * 2 + k) * 2 + y
    turn_a = [(number(y, k, x), number(x, k, y)) for x, k, y in devices]
    turn_b = [(number(y, k, 1 - x), number(x, k, y)) for x, k, y in devices]
    swap_core = [(r, r ^ 1) for r in range(n_row)]
    swap_col = [(0, 1), (1, 0)]
    pair = lambda step: [(l, l ^ step) for l in range(n_layer)]
    shift = lambda d: [(l, (l + d) % n_layer) for l in range(n_layer)]

    def call(kernel, outs, args, **extra):
        single = not isinstance(outs, list)
        return pl.pallas_call(
            kernel,
            out_shape=outs,
            in_specs=extra.pop("in_specs", [VMEM] * len(args)),
            out_specs=extra.pop("out_specs", VMEM if single else [VMEM] * len(outs)),
            compiler_params=LIMIT,
            **extra,
        )(*args)

    mask_t = a_mask[0].T
    b_first, b_rest, low = call(
        prepare_kernel,
        [
            shape((b_inner, tile, tile), bf16),
            shape((cols - 1, b_inner, tile, tile), bf16),
            shape((n_layer, half * tile, inner * tile), bf16),
        ],
        [pltpu.with_memory_space_constraint(x, pltpu.HBM) for x in (b_mask[0], mask_t, b_tiles, a_tiles)],
        in_specs=[pl.BlockSpec(memory_space=pltpu.HBM)] * 4,
        scratch_shapes=[
            pltpu.SMEM(b_mask.shape[1:], jnp.int32),
            pltpu.SMEM(mask_t.shape, jnp.int32),
            pltpu.VMEM(b_tiles.shape, bf16),
            pltpu.VMEM((n_layer, half, inner, tile, tile), bf16),
            pltpu.SemaphoreType.DMA((3 + n_layer,)),
        ],
    )

    def spread(block):
        r_a = lax.ppermute(block, ("row", "col"), turn_a)
        r_b = lax.ppermute(block, ("row", "col"), turn_b)
        return r_a, r_b

    def share(r_a, r_b):
        return r_a, r_b, lax.ppermute(r_a, "row", swap_core), lax.ppermute(r_b, "row", swap_core)

    turned = spread(b_first)
    turned_rest = spread(b_rest)
    first = share(*turned)
    rest = share(*turned_rest)

    def cost(rows):
        return pl.CostEstimate(
            flops=4 * n_layer * rows * inner * tile * tile,
            transcendentals=0,
            bytes_accessed=2 * n_layer * rows * inner * tile,
        )

    def batch(j):
        return (None, first) if j == 0 else (j - 1, rest)

    def product(unit):
        j, lo, n = unit
        at, blocks = batch(j)
        pieces = [(low, lo, min(lo + n, half)), (high, max(lo, half) - half, lo + n - half)]
        pieces = [(a, p * tile, q * tile) for a, p, q in pieces if a is not None and p < q]
        rows = n * tile
        return call(
            functools.partial(product_kernel, at, [piece[1:] for piece in pieces]),
            [shape((n_layer, rows + CODE_ROWS, tile), i16), shape((n_layer, rows, tile), f32)],
            [piece[0] for piece in pieces] + list(blocks),
            cost_estimate=cost(rows),
        )

    sent, own = {}, {}
    high = None
    coded, own["0"] = product(units["0"])
    sent["0"] = lax.ppermute(coded, "col", swap_col)
    late, _ = lax.optimization_barrier((a_tiles, coded))
    high = call(
        mask_high_kernel,
        shape((n_layer, half * tile, inner * tile), bf16),
        (mask_t, late),
        grid=(n_layer,),
        in_specs=[SMEM, pl.BlockSpec((None, half, inner, tile, tile), lambda t: (0, 2 * t + 1, 0, 0, 0))],
    )
    for u in list(units)[1:]:
        coded, own[u] = product(units[u])
        sent[u] = lax.ppermute(coded, "col", swap_col)

    squares, sums = {}, {}

    def add(u, kept, got):
        rows = kept.shape[0]
        last = u == final
        kernel, more, out = add_kernel, [], (1, tile)
        if last:
            order = list(sums)
            columns = [all_units[v][0] for v in order] + [all_units[u][0]]
            kernel, more = functools.partial(last_add_kernel, columns), [sums[v] for v in order]
            out = (n_row * n_layer, 8, tile)
        squares[u], sums[u] = call(kernel, [shape((rows, tile), f32), shape(out, f32)], [kept, *got, *more])

    all_units = units | {"z": layer_first}

    j, lo, n = layer_first
    rows = n * tile
    at, blocks = batch(j)
    kept, part = call(
        functools.partial(near_product_kernel, at),
        [shape((4, rows, tile), f32), shape((4, rows + CODE_ROWS, tile), i16)],
        [high, *blocks],
        cost_estimate=cost(rows),
    )
    part = lax.ppermute(part, "layer", pair(1))
    kept, part = call(
        far_product_kernel, [shape((2, rows, tile), f32), shape((2, rows + CODE_ROWS, tile), i16)], [kept, part]
    )
    part = lax.ppermute(part, "layer", pair(2))
    kept, part = call(finish_kernel, [shape((rows, tile), f32), shape((rows + CODE_ROWS, tile), i16)], [kept, part])
    add("z", kept, [lax.ppermute(part, "col", swap_col)])

    for u, (j, lo, n) in units.items():
        rows = n * tile
        block = shape((rows + CODE_ROWS, tile), i16)
        if u == final:
            kept, *parts = call(direct_kernel, [shape((rows, tile), f32)] + [block] * (n_layer - 1), [own[u], sent[u]])
            got = [lax.ppermute(part, "layer", shift(d)) for d, part in enumerate(parts, 1)]
        else:
            kept, part = call(
                split_kernel, [shape((2, rows, tile), f32), shape((2, rows + CODE_ROWS, tile), i16)], [own[u], sent[u]]
            )
            part = lax.ppermute(part, "layer", pair(1))
            kept, part = call(middle_kernel, [shape((rows, tile), f32), block], [kept, part])
            got = [lax.ppermute(part, "layer", pair(2))]
        add(u, kept, got)
    sums = sums[final]
    colsum = lax.all_to_all(sums, ("row", "layer"), 0, 0, tiled=True)
    return pl.pallas_call(
        functools.partial(final_kernel, [all_units[u] for u in squares], rows_total),
        out_shape=shape((tiles, cols, tile, tile), bf16),
        in_specs=[VMEM] * (1 + len(squares)),
        out_specs=pl.BlockSpec(memory_space=pl.ANY),
        scratch_shapes=[pltpu.VMEM((tiles, cols, tile, tile), bf16), pltpu.SemaphoreType.DMA((tiles,))],
        compiler_params=LIMIT,
        name="final",
    )(colsum, *squares.values())


def solution(mesh):
    n_row, n_col, n_layer = mesh.shape["row"], mesh.shape["col"], mesh.shape["layer"]

    def body(a_tiles, a_mask, b_tiles, b_mask):
        row_tiles, inner = a_tiles.shape[1:3]
        tiles = row_tiles // n_layer
        fits = (
            n_row == 4
            and n_col == 2
            and n_layer == 4
            and inner == 2 * b_tiles.shape[1]
            and tiles * n_layer == row_tiles
            and tiles <= CODE_ROWS
            and tiles % 4 == 0
            and b_tiles.shape[2] == 4
        )
        if fits:
            return coded_body(n_row, n_layer, a_tiles, a_mask, b_tiles, b_mask)
        return general_body(a_tiles, a_mask, b_tiles, b_mask)

    return jax.shard_map(
        body,
        mesh=mesh,
        in_specs=(
            P("layer", "row", "col", None, None),
            P("layer", "row", "col"),
            P("layer", "row", "col", None, None),
            P("layer", "row", "col"),
        ),
        out_specs=P(("row", "layer"), "col", None, None),
        check_vma=False,
    )
```

```python
import functools
import jax
import jax.numpy as jnp
from jax import lax
from jax.experimental import pallas as pl
from jax.experimental.pallas import tpu as pltpu
from jax.sharding import PartitionSpec as P


CODE_ROWS = 8
STEPS = 65000.0
MIDDLE = 32767
LOG_STEP = 0.0027076061740622863


VMEM = pl.BlockSpec(memory_space=pltpu.VMEM)
SMEM = pl.BlockSpec(memory_space=pltpu.SMEM)
LIMIT = pltpu.CompilerParams(vmem_limit_bytes=24 << 20)


def general_body(a_tiles, a_mask, b_tiles, b_mask):
    a_eff = (a_tiles * a_mask.astype(jnp.bfloat16)[..., None, None])[0]
    b_eff = (b_tiles * b_mask.astype(jnp.bfloat16)[..., None, None])[0]
    row_tiles = a_eff.shape[0]
    tile_size = a_eff.shape[-1]
    b_whole = lax.all_gather(b_eff, "row", axis=0, tiled=True)
    product = jnp.einsum(
        "ikab,kjbc->ijac",
        lax.all_gather(a_eff, "col", axis=1, tiled=True),
        b_whole,
        preferred_element_type=jnp.float32,
    )
    rows_total = row_tiles * lax.axis_size("row") * tile_size
    owned = lax.psum_scatter(product, "layer", scatter_dimension=0, tiled=True)
    squared = owned * owned
    local_sums = jnp.sum(squared, axis=(0, 2))
    colsum = lax.psum(local_sums, ("row", "layer"))
    scaled = rows_total * squared / (colsum[None, :, None, :] + 1e-06)
    return scaled.astype(jnp.bfloat16)


def encode(p, out_ref):
    rows, tile = p.shape
    tiles = rows // tile
    p3 = p.reshape(tiles, tile, tile)
    top = jnp.maximum(jnp.max(p3, axis=1), 1e-30)
    code = jnp.ceil(jnp.log(top) * (1.0 / LOG_STEP))
    factor = jnp.exp(code * -LOG_STEP) * STEPS
    q = (p3 * factor[:, None, :] + 0.5).astype(jnp.int32) - MIDDLE
    out_ref[:rows, :] = q.reshape(rows, tile).astype(jnp.int16)
    code = code.astype(jnp.int32)
    if tiles < CODE_ROWS:
        code = jnp.concatenate([code, jnp.zeros((CODE_ROWS - tiles, tile), jnp.int32)], axis=0)
    out_ref[rows:, :] = code.astype(jnp.int16)


def decode(ref):
    tile = ref.shape[1]
    rows = ref.shape[0] - CODE_ROWS
    tiles = rows // tile
    code = ref[rows:, :].astype(jnp.int32)[:tiles].astype(jnp.float32)
    factor = jnp.exp(code * LOG_STEP) * (1.0 / STEPS)
    q = ref[:rows, :].astype(jnp.int32) + MIDDLE
    q3 = q.astype(jnp.float32).reshape(tiles, tile, tile)
    return (q3 * factor[:, None, :]).reshape(rows, tile)


def prepare_kernel(
    b_mask_ref, a_mask_ref, b_ref, a_ref, first_ref, rest_ref, low_ref, b_ones, a_ones, b_buffer, buffer, sems
):
    shards, half = buffer.shape[:2]
    tiles = a_ref.shape[1] // shards
    pairs = [(b_mask_ref, b_ones), (b_ref, b_buffer), (a_mask_ref, a_ones)]
    pairs += [(a_ref.at[0, pl.ds(t * tiles, half)], buffer.at[t]) for t in range(shards)]
    copies = [pltpu.make_async_copy(source, target, sems.at[n]) for n, (source, target) in enumerate(pairs)]
    for copy in copies:
        copy.start()
    _, inner, cols, tile, _ = b_ref.shape
    zero = jnp.zeros((tile, tile), jnp.bfloat16)
    copies[0].wait()
    copies[1].wait()
    for k in range(inner):
        for j in range(cols):
            value = jnp.where(b_ones[k, j] != 0, b_buffer[0, k, j], zero)
            if j == 0:
                first_ref[k] = value
            else:
                rest_ref[j - 1, k] = value
    copies[2].wait()
    for t, copy in enumerate(copies[3:]):
        copy.wait()
        mask_rows(a_ones, t * tiles, buffer.at[t], low_ref.at[t])


def mask_rows(mask_ref, base, a_ref, out_ref):
    tiles, inner, tile = a_ref.shape[0], a_ref.shape[1], a_ref.shape[3]
    zero = jnp.zeros((tile, tile), jnp.bfloat16)
    for i in range(tiles):
        for k in range(inner):
            value = jnp.where(mask_ref[k, base + i] != 0, a_ref[i, k], zero)
            out_ref[i * tile : (i + 1) * tile, k * tile : (k + 1) * tile] = value


def mask_high_kernel(mask_ref, a_ref, out_ref):
    half = a_ref.shape[0]
    t = pl.program_id(0)
    mask_rows(mask_ref, (2 * t + 1) * half, a_ref, out_ref.at[t])


def right_side(b_refs, j):
    half, core = lax.axis_index("row") // 2, lax.axis_index("row") % 2
    straight = half == lax.axis_index("col")
    blocks = [ref[j] if j is not None else ref[...] for ref in b_refs]
    r_a, r_b, o_a, o_b = blocks
    sides = []
    for mine, other in (
        (jnp.where(straight, r_b, r_a), jnp.where(straight, o_b, o_a)),
        (jnp.where(straight, r_a, r_b), jnp.where(straight, o_a, o_b)),
    ):
        low = jnp.where(core == 0, mine, other)
        high = jnp.where(core == 0, other, mine)
        both = jnp.concatenate([low, high], axis=0)
        sides.append(both.reshape(both.shape[0] * both.shape[1], both.shape[2]))
    return jnp.concatenate(sides, axis=1)


def rows_of(parts, t):
    values = [ref[t, lo:hi, :] for ref, lo, hi in parts]
    return values[0] if len(values) == 1 else jnp.concatenate(values, axis=0)


def product_kernel(j, ranges, *refs):
    n = len(ranges)
    a_refs, b_refs, (out_ref, own_ref) = refs[:n], refs[n : n + 4], refs[n + 4 :]
    shards, _, tile = own_ref.shape
    right = right_side(b_refs, j)
    for t in range(shards):
        left = rows_of([(ref, lo, hi) for ref, (lo, hi) in zip(a_refs, ranges)], t)
        p = jnp.dot(left, right, preferred_element_type=jnp.float32)
        encode(p[:, :tile], out_ref.at[t])
        own_ref[t] = p[:, tile:]


def near_product_kernel(j, lo, hi, a_ref, *refs):
    b_refs, (keep_ref, out_ref) = refs[:4], refs[4:]
    tile = keep_ref.shape[2]
    layer = lax.axis_index("layer")
    right = right_side(b_refs, j)
    for step in range(a_ref.shape[0]):
        p = jnp.dot(a_ref[layer ^ step, lo:hi, :], right, preferred_element_type=jnp.float32)
        for side in range(2):
            value = p[:, side * tile : (side + 1) * tile]
            at = (step // 2) * 2 + side
            if step % 2:
                encode(value, out_ref.at[at])
            else:
                keep_ref[at] = value


def far_product_kernel(keep_ref, in_ref, own_ref, out_ref):
    for side in range(2):
        own_ref[side] = keep_ref[side] + decode(in_ref.at[side])
        encode(keep_ref[2 + side] + decode(in_ref.at[2 + side]), out_ref.at[side])


def finish_kernel(own_ref, in_ref, keep_ref, out_ref):
    encode(own_ref[0] + decode(in_ref.at[0]), out_ref)
    keep_ref[...] = own_ref[1] + decode(in_ref.at[1])


def split_kernel(own_ref, in_ref, keep_ref, out_ref):
    layer = lax.axis_index("layer")
    for n, step in enumerate((0, 2)):
        keep_ref[n] = own_ref[layer ^ step] + decode(in_ref.at[layer ^ step])
    for n, step in enumerate((1, 3)):
        encode(own_ref[layer ^ step] + decode(in_ref.at[layer ^ step]), out_ref.at[n])


def middle_kernel(keep_ref, in_ref, own_ref, out_ref):
    own_ref[...] = keep_ref[0] + decode(in_ref.at[0])
    encode(keep_ref[1] + decode(in_ref.at[1]), out_ref)


def direct_kernel(own_ref, in_ref, keep_ref, *out_refs):
    shards = own_ref.shape[0]
    layer = lax.axis_index("layer")
    for d, ref in enumerate(out_refs, 1):
        t = lax.rem(layer + d, shards)
        encode(own_ref[t] + decode(in_ref.at[t]), ref)
    keep_ref[...] = own_ref[layer] + decode(in_ref.at[layer])


def add_kernel(own_ref, *refs):
    ins, (sq_ref, cs_ref) = refs[:-2], refs[-2:]
    p = own_ref[...]
    for ref in ins:
        p = p + decode(ref)
    sq = p * p
    sq_ref[...] = sq
    cs_ref[...] = jnp.sum(sq, axis=0, keepdims=True)


def last_add_kernel(columns, own_ref, *refs):
    n_sums = len(columns) - 1
    ins, sums, (sq_ref, cs_ref) = refs[: -2 - n_sums], refs[-2 - n_sums : -2], refs[-2:]
    p = own_ref[...]
    for ref in ins:
        p = p + decode(ref)
    sq = p * p
    sq_ref[...] = sq
    totals = {}
    for column, value in zip(columns, [ref[...] for ref in sums] + [jnp.sum(sq, axis=0, keepdims=True)]):
        totals[column] = totals[column] + value if column in totals else value
    copies, height, tile = cs_ref.shape
    lines = [totals[column] for column in sorted(totals)]
    lines.append(jnp.zeros((height - len(lines), tile), jnp.float32))
    cs_ref[...] = jnp.broadcast_to(jnp.concatenate(lines, axis=0)[None], (copies, height, tile))


def final_kernel(units, rows_total, cs_ref, *refs):
    ins, (out_ref, buffer, sems) = refs[:-3], refs[-3:]
    tiles, _, tile, _ = out_ref.shape
    factor = rows_total / (jnp.sum(cs_ref[...], axis=0) + 1e-6)
    copies = []
    for i in range(tiles):
        for (j, lo, n), ref in zip(units, ins):
            if lo <= i < lo + n:
                value = ref[(i - lo) * tile : (i - lo + 1) * tile, :] * factor[j : j + 1, :]
                buffer[i, j] = value.astype(jnp.bfloat16)
        copies.append(pltpu.make_async_copy(buffer.at[i], out_ref.at[i], sems.at[i]))
        copies[-1].start()
    for copy in copies:
        copy.wait()


def coded_body(n_row, n_layer, a_tiles, a_mask, b_tiles, b_mask):
    _, row_tiles, inner, tile, _ = a_tiles.shape
    b_inner, cols = b_tiles.shape[1:3]
    tiles = row_tiles // n_layer
    rows_total = float(row_tiles * n_row * tile)
    f32, bf16, i16 = jnp.float32, jnp.bfloat16, jnp.int16
    shape = jax.ShapeDtypeStruct

    half, quarter, last_col = tiles // 2, tiles // 4, cols - 1
    units = {"0": (0, 0, half)}
    for j in range(1, last_col):
        units |= {str(2 * j - 1): (j, 0, half), str(2 * j): (j, half, half)}
    units |= {str(5 + q): (last_col, q * quarter, quarter) for q in range(3)}
    layer_first = {"z": (0, half, half), "w": (last_col, half + quarter, quarter)}
    final = "7"

    devices = [(x, k, y) for x in range(2) for k in range(2) for y in range(2)]
    number = lambda x, k, y: (x * 2 + k) * 2 + y
    turn_a = [(number(y, k, x), number(x, k, y)) for x, k, y in devices]
    turn_b = [(number(y, k, 1 - x), number(x, k, y)) for x, k, y in devices]
    swap_core = [(r, r ^ 1) for r in range(n_row)]
    swap_col = [(0, 1), (1, 0)]
    pair = lambda step: [(l, l ^ step) for l in range(n_layer)]
    shift = lambda d: [(l, (l + d) % n_layer) for l in range(n_layer)]

    def call(kernel, outs, args, **extra):
        single = not isinstance(outs, list)
        return pl.pallas_call(
            kernel,
            out_shape=outs,
            in_specs=extra.pop("in_specs", [VMEM] * len(args)),
            out_specs=extra.pop("out_specs", VMEM if single else [VMEM] * len(outs)),
            compiler_params=LIMIT,
            **extra,
        )(*args)

    mask_t = a_mask[0].T
    b_first, b_rest, low = call(
        prepare_kernel,
        [
            shape((b_inner, tile, tile), bf16),
            shape((cols - 1, b_inner, tile, tile), bf16),
            shape((n_layer, half * tile, inner * tile), bf16),
        ],
        [pltpu.with_memory_space_constraint(x, pltpu.HBM) for x in (b_mask[0], mask_t, b_tiles, a_tiles)],
        in_specs=[pl.BlockSpec(memory_space=pltpu.HBM)] * 4,
        scratch_shapes=[
            pltpu.SMEM(b_mask.shape[1:], jnp.int32),
            pltpu.SMEM(mask_t.shape, jnp.int32),
            pltpu.VMEM(b_tiles.shape, bf16),
            pltpu.VMEM((n_layer, half, inner, tile, tile), bf16),
            pltpu.SemaphoreType.DMA((3 + n_layer,)),
        ],
    )

    def spread(block):
        r_a = lax.ppermute(block, ("row", "col"), turn_a)
        r_b = lax.ppermute(block, ("row", "col"), turn_b)
        return r_a, r_b

    def share(r_a, r_b):
        return r_a, r_b, lax.ppermute(r_a, "row", swap_core), lax.ppermute(r_b, "row", swap_core)

    turned = spread(b_first)
    turned_rest = spread(b_rest)
    first = share(*turned)
    rest = share(*turned_rest)

    def cost(rows):
        return pl.CostEstimate(
            flops=4 * n_layer * rows * inner * tile * tile,
            transcendentals=0,
            bytes_accessed=2 * n_layer * rows * inner * tile,
        )

    def batch(j):
        return (None, first) if j == 0 else (j - 1, rest)

    def product(unit):
        j, lo, n = unit
        at, blocks = batch(j)
        pieces = [(low, lo, min(lo + n, half)), (high, max(lo, half) - half, lo + n - half)]
        pieces = [(a, p * tile, q * tile) for a, p, q in pieces if a is not None and p < q]
        rows = n * tile
        return call(
            functools.partial(product_kernel, at, [piece[1:] for piece in pieces]),
            [shape((n_layer, rows + CODE_ROWS, tile), i16), shape((n_layer, rows, tile), f32)],
            [piece[0] for piece in pieces] + list(blocks),
            cost_estimate=cost(rows),
        )

    sent, own = {}, {}
    high = None
    coded, own["0"] = product(units["0"])
    sent["0"] = lax.ppermute(coded, "col", swap_col)
    late, _ = lax.optimization_barrier((a_tiles, coded))
    high = call(
        mask_high_kernel,
        shape((n_layer, half * tile, inner * tile), bf16),
        (mask_t, late),
        grid=(n_layer,),
        in_specs=[SMEM, pl.BlockSpec((None, half, inner, tile, tile), lambda t: (0, 2 * t + 1, 0, 0, 0))],
    )
    for u in list(units)[1:]:
        coded, own[u] = product(units[u])
        sent[u] = lax.ppermute(coded, "col", swap_col)

    squares, sums = {}, {}

    def add(u, kept, got):
        rows = kept.shape[0]
        last = u == final
        kernel, more, out = add_kernel, [], (1, tile)
        if last:
            order = list(sums)
            columns = [all_units[v][0] for v in order] + [all_units[u][0]]
            kernel, more = functools.partial(last_add_kernel, columns), [sums[v] for v in order]
            out = (n_row * n_layer, 8, tile)
        squares[u], sums[u] = call(kernel, [shape((rows, tile), f32), shape(out, f32)], [kept, *got, *more])

    all_units = units | layer_first

    for u, (j, lo, n) in layer_first.items():
        rows = n * tile
        coded = lambda k: shape((k, rows + CODE_ROWS, tile), i16)
        at, blocks = batch(j)
        lo = (lo - half) * tile
        kept, part = call(
            functools.partial(near_product_kernel, at, lo, lo + rows),
            [shape((4, rows, tile), f32), coded(4)],
            [high, *blocks],
            cost_estimate=cost(rows),
        )
        part = lax.ppermute(part, "layer", pair(1))
        kept, part = call(far_product_kernel, [shape((2, rows, tile), f32), coded(2)], [kept, part])
        part = lax.ppermute(part, "layer", pair(2))
        kept, part = call(finish_kernel, [shape((rows, tile), f32), shape((rows + CODE_ROWS, tile), i16)], [kept, part])
        add(u, kept, [lax.ppermute(part, "col", swap_col)])

    for u, (j, lo, n) in units.items():
        rows = n * tile
        block = shape((rows + CODE_ROWS, tile), i16)
        if u == final:
            kept, *parts = call(direct_kernel, [shape((rows, tile), f32)] + [block] * (n_layer - 1), [own[u], sent[u]])
            got = [lax.ppermute(part, "layer", shift(d)) for d, part in enumerate(parts, 1)]
        else:
            kept, part = call(
                split_kernel, [shape((2, rows, tile), f32), shape((2, rows + CODE_ROWS, tile), i16)], [own[u], sent[u]]
            )
            part = lax.ppermute(part, "layer", pair(1))
            kept, part = call(middle_kernel, [shape((rows, tile), f32), block], [kept, part])
            got = [lax.ppermute(part, "layer", pair(2))]
        add(u, kept, got)
    sums = sums[final]
    colsum = lax.all_to_all(sums, ("row", "layer"), 0, 0, tiled=True)
    return pl.pallas_call(
        functools.partial(final_kernel, [all_units[u] for u in squares], rows_total),
        out_shape=shape((tiles, cols, tile, tile), bf16),
        in_specs=[VMEM] * (1 + len(squares)),
        out_specs=pl.BlockSpec(memory_space=pl.ANY),
        scratch_shapes=[pltpu.VMEM((tiles, cols, tile, tile), bf16), pltpu.SemaphoreType.DMA((tiles,))],
        compiler_params=LIMIT,
        name="final",
    )(colsum, *squares.values())


def solution(mesh):
    n_row, n_col, n_layer = mesh.shape["row"], mesh.shape["col"], mesh.shape["layer"]

    def body(a_tiles, a_mask, b_tiles, b_mask):
        row_tiles, inner = a_tiles.shape[1:3]
        tiles = row_tiles // n_layer
        fits = (
            n_row == 4
            and n_col == 2
            and n_layer == 4
            and inner == 2 * b_tiles.shape[1]
            and tiles * n_layer == row_tiles
            and tiles <= CODE_ROWS
            and tiles % 4 == 0
            and b_tiles.shape[2] == 4
        )
        if fits:
            return coded_body(n_row, n_layer, a_tiles, a_mask, b_tiles, b_mask)
        return general_body(a_tiles, a_mask, b_tiles, b_mask)

    return jax.shard_map(
        body,
        mesh=mesh,
        in_specs=(
            P("layer", "row", "col", None, None),
            P("layer", "row", "col"),
            P("layer", "row", "col", None, None),
            P("layer", "row", "col"),
        ),
        out_specs=P(("row", "layer"), "col", None, None),
        check_vma=False,
    )
```
